32 devices in a mesh: pole: 4 (over z), row: 4 (over y, x), col: 2 (over core).
Axes of the slice: x: 2, y: 2, z: 4, core: 2. Of those that a mesh axis runs over, the one named last changes fastest.
Arguments:
- green_blocks: bfloat16 [16, 2, 192, 1536], P('pole', 'col', None, 'row'), parts along dimension 0, may hold values from -0.15625 to 0.15625
- lower_panel: bfloat16 [1536, 32, 128], P(('row', 'col'), 'pole'), parts along dimension 1, may hold values from -1.5 to 1.5
- pattern: int32 [12, 8], replicated, may hold values 0 or 1
- pivot_inverse: float32 [8, 512, 128], P(('row', 'col'), 'pole'), parts along dimension 1, may hold values from -6 to 6
Outputs:
- green_panel: bfloat16 [6144, 8, 128], P('pole', ('row', 'col')), parts along dimension 0
- green_diag: float32 [8, 512, 128], P(('row', 'col'), 'pole'), parts along dimension 1
The draws below stay inside these ranges and needn't reach their ends.
There are 4 independent parts, one for each index of `pole`. The reference program is written for one: setup_inputs(seed, part) draws one part's arguments, and reference() takes and returns one part's arrays. A program takes and returns all parts, laid end to end along the dimension named above; an argument that names none is the same for every part. Nothing has to cross between parts.
All inputs are finite; a program needn't handle non-finite values.
Results may differ from the reference program's by a relative error of at most 0.01.
Values may be sent and summed in bfloat16 or wider, within the bound.
A program may use at most 128 MiB of HBM per device.

```python
import jax
import jax.numpy as jnp
from jax import lax

BLK = 128
RDEV = 192
ORDER = 1536
NBLK = 12
NK = 8
N_ROW = 4
N_COL = 2


def place_ends(values, own_key, low, top_value):
    spot = [jax.random.randint(jax.random.fold_in(own_key, axis), (), 0, length) for axis, length in enumerate(values.shape)]
    main_axis = values.shape.index(max(values.shape))
    beside = spot[:main_axis] + [(spot[main_axis] + 1) % values.shape[main_axis]] + spot[main_axis + 1:]
    return values.at[tuple(spot)].set(low).at[tuple(beside)].set(top_value)


def with_spikes(array, own_key, source, target, blocks, factor):
    def block_of(dim):
        return (jnp.arange(array.shape[dim]) // (array.shape[dim] // blocks)).reshape((-1,) + (1,) * (array.ndim - 1 - dim))

    first = jax.random.permutation(own_key, blocks)[block_of(target)]
    far = (block_of(target) + blocks // 2) % blocks
    return jnp.where((block_of(source) == first) | (block_of(source) == far), factor * array, array)


def steps_of(own_key, shape, shards, least, top_value):
    level = 1.0
    for position, shards_of in shards:
        steps = jax.random.uniform(jax.random.fold_in(jax.random.fold_in(own_key, 6), position), (shards_of,), jnp.float32, least / len(shards), top_value / len(shards))
        level = level * jnp.repeat(jnp.exp(steps), shape[position] // shards_of).reshape((-1,) + (1,) * (len(shape) - 1 - position))
    return level


def scatter_about(key, shape, spread, reach, cuts=(), dtype=jnp.bfloat16):
    drawn = jax.random.normal(key, shape, jnp.float32) * spread
    if len(cuts) > 0:
        drawn = steps_of(key, shape, cuts, -0.22, 0.18) * drawn
    return jnp.clip(drawn, min=-reach, max=reach).astype(dtype)


def gaussian_with(rng, extent, spread, bound, cuts, heavy, kind=jnp.bfloat16):
    values = spread * jax.random.normal(rng, extent, jnp.float32)
    if cuts:
        values = values * steps_of(rng, extent, cuts, -0.22, 0.18)
    return jnp.clip(with_spikes(values, jax.random.fold_in(rng, 3), *heavy), -bound, bound).astype(kind)


def setup_inputs(seed: int = 0, part: int = 0) -> dict:
    seeds = jax.random.split(jax.random.key(seed), 5)
    own_keys = jax.random.split(jax.random.fold_in(seeds[4], part), 5)
    green_blocks = scatter_about(own_keys[0], (N_ROW, N_COL, RDEV, ORDER), ORDER ** -0.5, 0.15625, ((1, 2), (3, 4)))
    lower_panel = gaussian_with(own_keys[1], (ORDER, NK, BLK), 0.25, 1.5, ((0, 8),), (0, 1, 8, 2.0))
    pattern = place_ends((jax.random.randint(seeds[2], (NBLK, NK), 0, 2) < 1).astype(jnp.int32), jax.random.fold_in(seeds[2], 1), 0, 1)
    pivot_inverse = scatter_about(own_keys[3], (NK, BLK, BLK), 1.0, 6.0, ((0, 8),), jnp.float32)
    return dict(green_blocks=green_blocks, lower_panel=lower_panel, pattern=pattern, pivot_inverse=pivot_inverse)


def reference(green_blocks, lower_panel, pattern, pivot_inverse):
    matrix = green_blocks.reshape(ORDER, ORDER)
    row_mask = jnp.repeat(pattern, BLK, axis=0)
    masked = lower_panel * row_mask[:, :, None].astype(jnp.bfloat16)
    flat = masked.reshape(ORDER, NK * BLK)
    span = ORDER // N_ROW
    product = jnp.zeros((ORDER, NK * BLK), jnp.float32)
    for index in range(N_ROW):
        piece = jnp.dot(matrix[:, index * span:(index + 1) * span], flat[index * span:(index + 1) * span], preferred_element_type=jnp.float32)
        rounded = lax.optimization_barrier(piece.astype(jnp.bfloat16))
        product = product + rounded.astype(jnp.float32)
    resolved = product.reshape(ORDER, NK, BLK)
    green_panel = (-(resolved * row_mask[:, :, None].astype(jnp.float32))).astype(jnp.bfloat16)
    green_diag = pivot_inverse + jnp.einsum("rkb,rkc->kbc", masked.astype(jnp.float32), resolved, precision=lax.Precision.HIGHEST)
    return green_panel, green_diag
```

```python
import functools

import jax
import jax.numpy as jnp
from jax import lax
from jax.experimental import pallas as pl
from jax.experimental.pallas import tpu as pltpu
from jax.sharding import PartitionSpec as P

MESH = pl.DeviceIdType.MESH
PAIR = 2


def kernel(
    rows, cols, pattern_ref, green_ref, panel_ref, pivot_ref, out_ref, diag_ref,
    slab, column, to_far, from_far, to_x, to_y, to_own, from_own, from_x, from_y,
    slab_send, slab_recv, column_send, column_recv, far_send, far_recv,
    x_send, x_recv, y_send, y_recv, own_send, own_recv,
):
    r, c = lax.axis_index("row"), lax.axis_index("col")
    me = r * cols + c
    share, width = panel_ref.shape[1:]
    half = rows // 2 * share
    row_x, row_y, row_far = r + 1 - 2 * (r % 2), (r + 2) % 4, 3 - r
    halves = (slice(0, half), slice(half, 2 * half))

    def remote(src, dst, send, recv, row, col):
        return pltpu.make_async_remote_copy(
            src_ref=src, dst_ref=dst, send_sem=send, recv_sem=recv,
            device_id={"row": row, "col": col}, device_id_type=MESH,
        )

    barrier = pltpu.get_barrier_semaphore()
    for step in range(1, cols):
        pl.semaphore_signal(barrier, 1, device_id={"row": r, "col": (c + step) % cols}, device_id_type=MESH)
    for row in (row_x, row_y, row_far):
        for k in range(cols):
            pl.semaphore_signal(barrier, 1, device_id={"row": row, "col": k}, device_id_type=MESH)
    slab[c] = panel_ref[...]
    pl.semaphore_wait(barrier, rows * cols - 1)

    started = []

    def start(copy):
        copy.start()
        started.append(copy)

    for step in range(1, cols):
        k = (c + step) % cols
        start(remote(panel_ref, slab.at[c], slab_send.at[k], slab_recv.at[c], r, k))

    def send_column(d, row):
        for k in range(cols):
            start(remote(
                panel_ref.at[row * cols + k], column.at[me],
                column_send.at[d, k], column_recv.at[d, c], row, k,
            ))

    send_column(0, row_x)
    send_column(1, row_y)

    for step in range(1, cols):
        k = (c + step) % cols
        remote(panel_ref, slab.at[k], slab_send.at[k], slab_recv.at[k], r, k).wait_recv()

    chunk = cols * share // width

    def right(row, k):
        parts = []
        for p in range(PAIR):
            supernode = row * cols + k + p
            whole = jnp.concatenate([slab[s, supernode] for s in range(cols)], axis=0)
            blocks = []
            for q in range(chunk):
                flag = pattern_ref[r * chunk + q, supernode].astype(jnp.float32)
                blocks.append((whole[q * width:(q + 1) * width].astype(jnp.float32) * flag).astype(jnp.bfloat16))
            parts.append(jnp.concatenate(blocks, axis=0))
        return jnp.concatenate(parts, axis=1)

    def left(h):
        return green_ref[h * rows // 2:(h + 1) * rows // 2].reshape(half, green_ref.shape[2])

    def product(h, rhs):
        return jnp.dot(left(h), rhs, preferred_element_type=jnp.float32).astype(jnp.bfloat16)

    def over_pairs(body):
        if cols == PAIR:
            body(0)
        else:
            lax.fori_loop(0, cols // PAIR, lambda i, z: (body(i * PAIR), z)[1], 0)

    def far_body(k):
        rhs = right(row_far, k)
        for h in range(2):
            value = product(h, rhs)
            for p in range(PAIR):
                to_far[h, k + p] = value[:, p * width:(p + 1) * width]

    def near_body(row, buffer):
        def body(k):
            rhs = right(row, k)
            for h in range(2):
                value = product(h, rhs)
                for p in range(PAIR):
                    buffer[k + p, halves[h]] = value[:, p * width:(p + 1) * width]
        return body

    over_pairs(far_body)
    start(remote(to_far.at[0], from_far.at[0], far_send.at[0], far_recv.at[0], row_x, c))
    start(remote(to_far.at[1], from_far.at[1], far_send.at[1], far_recv.at[1], row_y, c))

    def send_half(buffer, target, send, recv, h, row):
        for k in range(cols):
            start(remote(
                buffer.at[k, pl.ds(h * half, half)], target.at[c, pl.ds(h * half, half)],
                send.at[h, k], recv.at[h, c], row, k,
            ))

    over_pairs(near_body(row_x, to_x))
    send_half(to_x, from_x, x_send, x_recv, 0, row_x)
    over_pairs(near_body(row_y, to_y))
    send_half(to_y, from_y, y_send, y_recv, 1, row_y)
    send_column(2, row_far)
    over_pairs(near_body(r, to_own))
    for step in range(1, cols):
        k = (c + step) % cols
        start(remote(to_own.at[k], from_own.at[c], own_send.at[k], own_recv.at[c], r, k))
    from_own[c] = to_own[c]

    def add_half(buffer, h):
        for k in range(cols):
            total = buffer[k, halves[h]].astype(jnp.float32) + from_far[h, k].astype(jnp.float32)
            buffer[k, halves[h]] = total.astype(jnp.bfloat16)

    remote(to_far.at[0], from_far.at[0], far_send.at[0], far_recv.at[0], row_x, c).wait_recv()
    add_half(to_y, 0)
    send_half(to_y, from_y, y_send, y_recv, 0, row_y)
    remote(to_far.at[1], from_far.at[1], far_send.at[1], far_recv.at[1], row_y, c).wait_recv()
    add_half(to_x, 1)
    send_half(to_x, from_x, x_send, x_recv, 1, row_x)

    for s in range(cols):
        column[r * cols + s] = slab[s, me]
    for d, row in enumerate((row_x, row_y, row_far)):
        for k in range(cols):
            place = column.at[row * cols + k]
            remote(place, place, column_send.at[d, k], column_recv.at[d, k], row, k).wait_recv()
    for step in range(1, cols):
        k = (c + step) % cols
        remote(to_own.at[k], from_own.at[k], own_send.at[k], own_recv.at[k], r, k).wait_recv()

    def wait_half(target, send, recv, h, row):
        for k in range(cols):
            place = target.at[k, pl.ds(h * half, half)]
            remote(place, place, send.at[h, k], recv.at[h, k], row, k).wait_recv()

    def finish(j):
        span = slice(j * share, (j + 1) * share)
        value = jnp.concatenate(
            [
                from_own[s, span].astype(jnp.float32)
                + from_x[s, span].astype(jnp.float32)
                + from_y[s, span].astype(jnp.float32)
                for s in range(cols)
            ],
            axis=0,
        )
        panel = jnp.concatenate([column[j * cols + s] for s in range(cols)], axis=0)
        blocks = []
        for q in range(chunk):
            flag = pattern_ref[j * chunk + q, me].astype(jnp.float32)
            part = slice(q * width, (q + 1) * width)
            begin = j * chunk * width + q * width
            out_ref[begin:begin + width] = (-(value[part] * flag)).astype(jnp.bfloat16)
            blocks.append((panel[part].astype(jnp.float32) * flag).astype(jnp.bfloat16))
        masked = jnp.concatenate(blocks, axis=0)
        high = value.astype(jnp.bfloat16)
        low = (value - high.astype(jnp.float32)).astype(jnp.bfloat16)
        both = lax.dot_general(
            masked, jnp.concatenate([high, low], axis=1), (((0,), (0,)), ((), ())),
            preferred_element_type=jnp.float32,
        )
        return both[:, :width] + both[:, width:]

    total = pivot_ref[...]
    for h in range(2):
        wait_half(from_x, x_send, x_recv, h, row_x)
        wait_half(from_y, y_send, y_recv, h, row_y)
        for j in range(h * rows // 2, (h + 1) * rows // 2):
            total = total + finish(j)
    diag_ref[...] = total
    for copy in started:
        copy.wait_send()


def local(green_blocks, lower_panel, pattern, pivot_inverse):
    rows, cols = lax.axis_size("row"), lax.axis_size("col")
    share, supernodes, width = lower_panel.shape
    tall = rows * share
    vmem = pl.BlockSpec(memory_space=pltpu.VMEM)
    bf16 = lambda *shape: pltpu.VMEM(shape, jnp.bfloat16)
    dma = lambda *shape: pltpu.SemaphoreType.DMA(shape)
    out, diag = pl.pallas_call(
        functools.partial(kernel, rows, cols),
        out_shape=(
            jax.ShapeDtypeStruct((tall * cols, width), jnp.bfloat16),
            jax.ShapeDtypeStruct((width, width), jnp.float32),
        ),
        in_specs=[pl.BlockSpec(memory_space=pltpu.SMEM), vmem, vmem, vmem],
        out_specs=(vmem, vmem),
        scratch_shapes=[
            bf16(cols, supernodes, share, width),
            bf16(rows * cols, share, width),
            bf16(2, cols, tall // 2, width),
            bf16(2, cols, tall // 2, width),
            bf16(cols, tall, width),
            bf16(cols, tall, width),
            bf16(cols, tall, width),
            bf16(cols, tall, width),
            bf16(cols, tall, width),
            bf16(cols, tall, width),
            dma(cols), dma(cols), dma(3, cols), dma(3, cols), dma(2), dma(2),
            dma(2, cols), dma(2, cols), dma(2, cols), dma(2, cols), dma(cols), dma(cols),
        ],
        compiler_params=pltpu.CompilerParams(
            collective_id=0, has_side_effects=True, vmem_limit_bytes=60 * 1024 * 1024,
        ),
    )(
        pattern,
        green_blocks.reshape(rows, share, -1),
        lower_panel.transpose(1, 0, 2),
        pivot_inverse.reshape(width, width),
    )
    return out.reshape(-1, 1, width), diag.reshape(1, width, width)


def solution(mesh):
    placed = (
        P("pole", "col", None, "row"),
        P(("row", "col"), "pole", None),
        P(),
        P(("row", "col"), "pole", None),
    )
    return jax.shard_map(
        local,
        mesh=mesh,
        in_specs=placed,
        out_specs=(P("pole", ("row", "col"), None), P(("row", "col"), "pole", None)),
        check_vma=False,
    )
```

```python
import functools
import math

import jax
import jax.numpy as jnp
from jax import lax
from jax.experimental import pallas as pl
from jax.experimental.pallas import tpu as pltpu
from jax.sharding import PartitionSpec as P

MESH = pl.DeviceIdType.MESH
PAIR = 2


def exchange(
    rows, cols, pattern_hbm, green_hbm, panel_hbm, pivot_hbm,
    base, last, column, diag_ref, flags,
    pattern_ref, green_ref, panel_ref, wide, pivot_ref, slab, to_far, from_far, to_x, to_y, to_own, from_own, from_x, from_y,
    load, slab_send, slab_recv, column_send, column_recv, far_send, far_recv,
    x_send, x_recv, y_send, y_recv, own_send, own_recv,
):
    r, c = lax.axis_index("row"), lax.axis_index("col")
    me = r * cols + c
    share, supernodes, width = panel_ref.shape
    mid = rows // 2
    half = mid * share
    row_x, row_y, row_far = r + 1 - 2 * (r % 2), (r + 2) % 4, 3 - r

    def remote(src, dst, send, recv, row, col):
        return pltpu.make_async_remote_copy(
            src_ref=src, dst_ref=dst, send_sem=send, recv_sem=recv,
            device_id={"row": row, "col": col}, device_id_type=MESH,
        )

    barrier = pltpu.get_barrier_semaphore()
    for row in (row_far, row_x, row_y):
        for k in range(cols):
            pl.semaphore_signal(barrier, 1, device_id={"row": row, "col": k}, device_id_type=MESH)
    for step in range(1, cols):
        pl.semaphore_signal(barrier, 1, device_id={"row": r, "col": (c + step) % cols}, device_id_type=MESH)
    loads = [
        pltpu.make_async_copy(panel_hbm, panel_ref, load.at[0]),
        pltpu.make_async_copy(green_hbm, green_ref, load.at[1]),
        pltpu.make_async_copy(pivot_hbm, pivot_ref, load.at[2]),
        pltpu.make_async_copy(pattern_hbm, pattern_ref, load.at[3]),
    ]
    for copy in loads:
        copy.start()

    loads[0].wait()
    loads[3].wait()
    wide[...] = panel_ref[...].astype(jnp.float32).reshape(share * supernodes, width)
    piece = math.gcd(share, width)
    for k in range(supernodes):
        value = wide[pl.ds(k, share, stride=supernodes), :]
        parts = []
        for q in range(share // piece):
            flag = pattern_ref[k, (me * share + q * piece) // width].astype(jnp.float32)
            parts.append(value[q * piece:(q + 1) * piece] * flag)
        slab[c, k] = jnp.concatenate(parts, axis=0).astype(jnp.bfloat16)
    pl.semaphore_wait(barrier, rows * cols - 1)

    started = []

    def start(copy):
        copy.start()
        started.append(copy)

    for step in range(1, cols):
        k = (c + step) % cols
        start(remote(slab.at[c], slab.at[c], slab_send.at[k], slab_recv.at[c], r, k))

    def send_column(d, row):
        for k in range(cols):
            start(remote(
                slab.at[c, row * cols + k], column.at[me],
                column_send.at[d, k], column_recv.at[d, c], row, k,
            ))

    send_column(0, row_x)
    send_column(1, row_y)
    loads[1].wait()

    for step in range(1, cols):
        k = (c + step) % cols
        remote(slab.at[k], slab.at[k], slab_send.at[k], slab_recv.at[k], r, k).wait_recv()

    def product(h, row, k):
        rhs = jnp.concatenate(
            [
                jnp.concatenate([slab[s, row * cols + k + p] for s in range(cols)], axis=0)
                for p in range(PAIR)
            ],
            axis=1,
        )
        lhs = green_ref[h * mid:(h + 1) * mid].reshape(half, green_ref.shape[2])
        value = jnp.dot(lhs, rhs, preferred_element_type=jnp.float32).astype(jnp.bfloat16)
        return value.reshape(mid, share, PAIR * width)

    def fill(buffer, h, row, offset):
        def body(k):
            value = product(h, row, k)
            for p in range(PAIR):
                buffer[k + p, offset:offset + mid] = value[:, :, p * width:(p + 1) * width]

        if cols == PAIR:
            body(0)
        else:
            lax.fori_loop(0, cols // PAIR, lambda i, z: (body(i * PAIR), z)[1], 0)

    for h, row in enumerate((row_x, row_y)):
        fill(to_far.at[h], h, row_far, 0)
        start(remote(to_far.at[h], from_far.at[h], far_send.at[h], far_recv.at[h], row, c))

    def send_direct(buffer, target, send, recv, h, row):
        for k in range(cols):
            start(remote(
                buffer.at[k, pl.ds(h * mid, mid)], target.at[c],
                send.at[h, k], recv.at[h, c], row, k,
            ))

    def send_sum(buffer, send, recv, h, row):
        for k in range(cols):
            start(remote(
                buffer.at[k, pl.ds(h * mid, mid)], last.at[pl.ds(h * mid, mid), c],
                send.at[h, k], recv.at[h, c], row, k,
            ))

    fill(to_x, 0, row_x, 0)
    send_direct(to_x, from_x, x_send, x_recv, 0, row_x)
    fill(to_y, 1, row_y, mid)
    send_direct(to_y, from_y, y_send, y_recv, 1, row_y)
    send_column(2, row_far)
    fill(to_y, 0, row_y, 0)
    fill(to_x, 1, row_x, mid)
    for h in range(2):
        fill(to_own, h, r, h * mid)
    for step in range(1, cols):
        k = (c + step) % cols
        start(remote(to_own.at[k], from_own.at[c], own_send.at[k], own_recv.at[c], r, k))
    from_own[c] = to_own[c]

    for h, row, buffer, send, recv, target in (
        (0, row_x, to_y, y_send, y_recv, row_y), (1, row_y, to_x, x_send, x_recv, row_x)
    ):
        remote(to_far.at[h], from_far.at[h], far_send.at[h], far_recv.at[h], row, c).wait_recv()
        for k in range(cols):
            span = slice(h * mid, (h + 1) * mid)
            total = buffer[k, span].astype(jnp.float32) + from_far[h, k].astype(jnp.float32)
            buffer[k, span] = total.astype(jnp.bfloat16)
        send_sum(buffer, send, recv, h, target)

    for s in range(cols):
        column[r * cols + s] = slab[s, me]
    for i in range(flags.shape[0]):
        flags[i] = jnp.broadcast_to(pattern_ref[me, i].astype(jnp.float32), flags.shape[1:])
    for d, row in enumerate((row_x, row_y, row_far)):
        for k in range(cols):
            place = column.at[row * cols + k]
            remote(place, place, column_send.at[d, k], column_recv.at[d, k], row, k).wait_recv()
    for step in range(1, cols):
        k = (c + step) % cols
        remote(to_own.at[k], from_own.at[k], own_send.at[k], own_recv.at[k], r, k).wait_recv()
    loads[2].wait()
    grown = pivot_ref[...]
    for h, source, send, recv, row in ((0, from_x, x_send, x_recv, row_x), (1, from_y, y_send, y_recv, row_y)):
        for k in range(cols):
            remote(source.at[k], source.at[k], send.at[h, k], recv.at[h, k], row, k).wait_recv()
        for j in range(mid):
            panel = []
            value = []
            for s in range(cols):
                value.append(
                    from_own[s, h * mid + j].astype(jnp.float32) + source[s, j].astype(jnp.float32)
                )
                panel.append(column[(h * mid + j) * cols + s])
                base[h * mid + j, s] = value[-1]
            value = jnp.concatenate(value, axis=0)
            high = value.astype(jnp.bfloat16)
            low = (value - high.astype(jnp.float32)).astype(jnp.bfloat16)
            both = lax.dot_general(
                jnp.concatenate(panel, axis=0), jnp.concatenate([high, low], axis=1),
                (((0,), (0,)), ((), ())), preferred_element_type=jnp.float32,
            )
            grown = grown + (both[:, :width] + both[:, width:])
    diag_ref[...] = grown

    for h, send, recv, row in ((0, y_send, y_recv, row_y), (1, x_send, x_recv, row_x)):
        for k in range(cols):
            place = last.at[pl.ds(h * mid, mid), k]
            remote(place, place, send.at[h, k], recv.at[h, k], row, k).wait_recv()
    for copy in started:
        copy.wait_send()


def finish(base, last, column, grown, flags, out_ref, diag_ref):
    rows, cols, share, width = base.shape
    chunk = cols * share // width
    total = grown[...]
    for j in range(rows):
        late = last[j].reshape(cols * share, width)
        value = base[j].reshape(cols * share, width) + late.astype(jnp.float32)
        for q in range(chunk):
            begin = (j * chunk + q) * width
            part = value[q * width:(q + 1) * width] * flags[j * chunk + q, 0:1]
            out_ref[begin:begin + width] = (-part).astype(jnp.bfloat16)
        panel = column[j * cols:(j + 1) * cols].reshape(cols * share, width)
        total = total + lax.dot_general(
            panel, late, (((0,), (0,)), ((), ())), preferred_element_type=jnp.float32
        )
    diag_ref[...] = total


def local(green_blocks, lower_panel, pattern, pivot_inverse):
    rows, cols = lax.axis_size("row"), lax.axis_size("col")
    share, supernodes, width = lower_panel.shape
    blocks = pattern.shape[0]
    mid = rows // 2
    vmem = pl.BlockSpec(memory_space=pltpu.VMEM)
    hbm = pl.BlockSpec(memory_space=pltpu.HBM)
    bf16 = lambda *shape: pltpu.VMEM(shape, jnp.bfloat16)
    dma = lambda *shape: pltpu.SemaphoreType.DMA(shape)
    green = green_blocks.reshape(rows, share, -1)
    buffers = [
        bf16(*green.shape),
        bf16(*lower_panel.shape),
        pltpu.VMEM((share * supernodes, width), jnp.float32),
        pltpu.VMEM((width, width), jnp.float32),
        bf16(cols, supernodes, share, width),
        bf16(2, cols, mid, share, width),
        bf16(2, cols, mid, share, width),
        bf16(cols, rows, share, width),
        bf16(cols, rows, share, width),
        bf16(cols, rows, share, width),
        bf16(cols, rows, share, width),
        bf16(cols, mid, share, width),
        bf16(cols, mid, share, width),
    ]
    held = sum(math.prod(b.shape) * jnp.dtype(b.dtype).itemsize for b in buffers)
    middle = pl.pallas_call(
        functools.partial(exchange, rows, cols),
        out_shape=(
            pltpu.VMEM((rows, cols, share, width), jnp.float32),
            pltpu.VMEM((rows, cols, share, width), jnp.bfloat16),
            pltpu.VMEM((rows * cols, share, width), jnp.bfloat16),
            pltpu.VMEM((width, width), jnp.float32),
            pltpu.VMEM((blocks, 8, width), jnp.float32),
        ),
        in_specs=[hbm] * 4,
        out_specs=(vmem,) * 5,
        scratch_shapes=[pltpu.SMEM(pattern.shape[::-1], pattern.dtype)] + buffers + [
            dma(4), dma(cols), dma(cols), dma(3, cols), dma(3, cols), dma(2), dma(2),
            dma(2, cols), dma(2, cols), dma(2, cols), dma(2, cols), dma(cols), dma(cols),
        ],
        compiler_params=pltpu.CompilerParams(
            collective_id=0, has_side_effects=True, vmem_limit_bytes=held + held // 4 + 4 * 1024 * 1024,
        ),
    )(*(pltpu.with_memory_space_constraint(a, pltpu.HBM) for a in (pattern.T, green, lower_panel, pivot_inverse.reshape(width, width))))
    out, diag = pl.pallas_call(
        finish,
        out_shape=(
            jax.ShapeDtypeStruct((rows * cols * share, width), jnp.bfloat16),
            jax.ShapeDtypeStruct((width, width), jnp.float32),
        ),
        in_specs=[vmem] * 5,
        out_specs=(vmem, vmem),
        compiler_params=pltpu.CompilerParams(vmem_limit_bytes=16 * 1024 * 1024),
    )(*middle)
    return out.reshape(-1, 1, width), diag.reshape(1, width, width)


def solution(mesh):
    placed = (
        P("pole", "col", None, "row"),
        P(("row", "col"), "pole", None),
        P(),
        P(("row", "col"), "pole", None),
    )
    return jax.shard_map(
        local,
        mesh=mesh,
        in_specs=placed,
        out_specs=(P("pole", ("row", "col"), None), P(("row", "col"), "pole", None)),
        check_vma=False,
    )
```

```python
import functools
import math

import jax
import jax.numpy as jnp
from jax import lax
from jax.experimental import pallas as pl
from jax.experimental.pallas import tpu as pltpu
from jax.sharding import PartitionSpec as P

MESH = pl.DeviceIdType.MESH
PAIR = 2


def exchange(
    rows, cols, pattern_hbm, green_hbm, panel_hbm, pivot_hbm,
    base, last, column, diag_ref, flags,
    pattern_ref, green_ref, panel_ref, wide, pivot_ref, slab, to_far, from_far, to_x, to_y, to_own, from_own, from_x, from_y,
    load, slab_send, slab_recv, column_send, column_recv, far_send, far_recv,
    x_send, x_recv, y_send, y_recv, own_send, own_recv,
):
    r, c = lax.axis_index("row"), lax.axis_index("col")
    me = r * cols + c
    share, supernodes, width = panel_ref.shape
    mid = rows // 2
    half = mid * share
    row_x, row_y, row_far = r + 1 - 2 * (r % 2), (r + 2) % 4, 3 - r

    def remote(src, dst, send, recv, row, col):
        return pltpu.make_async_remote_copy(
            src_ref=src, dst_ref=dst, send_sem=send, recv_sem=recv,
            device_id={"row": row, "col": col}, device_id_type=MESH,
        )

    barrier = pltpu.get_barrier_semaphore()
    for row in (row_x, row_y):
        for k in range(cols):
            pl.semaphore_signal(barrier, 1, device_id={"row": row, "col": k}, device_id_type=MESH)
    for step in range(1, cols):
        pl.semaphore_signal(barrier, 1, device_id={"row": r, "col": (c + step) % cols}, device_id_type=MESH)
    loads = [
        pltpu.make_async_copy(panel_hbm, panel_ref, load.at[0]),
        pltpu.make_async_copy(green_hbm, green_ref, load.at[1]),
        pltpu.make_async_copy(pivot_hbm, pivot_ref, load.at[2]),
        pltpu.make_async_copy(pattern_hbm, pattern_ref, load.at[3]),
    ]
    for copy in loads:
        copy.start()

    loads[0].wait()
    loads[3].wait()
    wide[...] = panel_ref[...].astype(jnp.float32).reshape(share * supernodes, width)
    piece = math.gcd(share, width)
    for k in range(supernodes):
        value = wide[pl.ds(k, share, stride=supernodes), :]
        parts = []
        for q in range(share // piece):
            flag = pattern_ref[k, (me * share + q * piece) // width].astype(jnp.float32)
            parts.append(value[q * piece:(q + 1) * piece] * flag)
        slab[c, k] = jnp.concatenate(parts, axis=0).astype(jnp.bfloat16)
    pl.semaphore_wait(barrier, 3 * cols - 1)

    started = []

    def start(copy):
        copy.start()
        started.append(copy)

    for step in range(1, cols):
        k = (c + step) % cols
        start(remote(slab.at[c], slab.at[c], slab_send.at[k], slab_recv.at[c], r, k))

    def send_column(d, row):
        for k in range(cols):
            start(remote(
                slab.at[c, row * cols + k], column.at[me],
                column_send.at[d, k], column_recv.at[d, c], row, k,
            ))

    send_column(0, row_x)
    send_column(1, row_y)
    loads[1].wait()

    for step in range(1, cols):
        k = (c + step) % cols
        remote(slab.at[k], slab.at[k], slab_send.at[k], slab_recv.at[k], r, k).wait_recv()

    def product(h, row, k):
        rhs = jnp.concatenate(
            [
                jnp.concatenate([slab[s, row * cols + k + p] for s in range(cols)], axis=0)
                for p in range(PAIR)
            ],
            axis=1,
        )
        lhs = green_ref[h * mid:(h + 1) * mid].reshape(half, green_ref.shape[2])
        value = jnp.dot(lhs, rhs, preferred_element_type=jnp.float32).astype(jnp.bfloat16)
        return value.reshape(mid, share, PAIR * width)

    def fill(buffer, h, row, offset):
        def body(k):
            value = product(h, row, k)
            for p in range(PAIR):
                buffer[k + p, offset:offset + mid] = value[:, :, p * width:(p + 1) * width]

        if cols == PAIR:
            body(0)
        else:
            lax.fori_loop(0, cols // PAIR, lambda i, z: (body(i * PAIR), z)[1], 0)

    for h, row in enumerate((row_x, row_y)):
        fill(to_far.at[h], h, row_far, 0)
        start(remote(to_far.at[h], from_far.at[h], far_send.at[h], far_recv.at[h], row, c))

    def send_direct(buffer, target, send, recv, h, row):
        for k in range(cols):
            start(remote(
                buffer.at[k, pl.ds(h * mid, mid)], target.at[c],
                send.at[h, k], recv.at[h, c], row, k,
            ))

    def send_sum(buffer, send, recv, h, row):
        for k in range(cols):
            start(remote(
                buffer.at[k, pl.ds(h * mid, mid)], last.at[pl.ds(h * mid, mid), c],
                send.at[h, k], recv.at[h, c], row, k,
            ))

    fill(to_x, 0, row_x, 0)
    send_direct(to_x, from_x, x_send, x_recv, 0, row_x)
    fill(to_y, 1, row_y, mid)
    send_direct(to_y, from_y, y_send, y_recv, 1, row_y)
    fill(to_y, 0, row_y, 0)
    fill(to_x, 1, row_x, mid)
    for h in range(2):
        fill(to_own, h, r, h * mid)
    for step in range(1, cols):
        k = (c + step) % cols
        start(remote(to_own.at[k], from_own.at[c], own_send.at[k], own_recv.at[c], r, k))
    from_own[c] = to_own[c]

    for h, row, buffer, send, recv, target in (
        (0, row_x, to_y, y_send, y_recv, row_y), (1, row_y, to_x, x_send, x_recv, row_x)
    ):
        remote(to_far.at[h], from_far.at[h], far_send.at[h], far_recv.at[h], row, c).wait_recv()
        if h == 0:
            send_column(2, row_far)
        for k in range(cols):
            span = slice(h * mid, (h + 1) * mid)
            total = buffer[k, span].astype(jnp.float32) + from_far[h, k].astype(jnp.float32)
            buffer[k, span] = total.astype(jnp.bfloat16)
        send_sum(buffer, send, recv, h, target)

    for s in range(cols):
        column[r * cols + s] = slab[s, me]
    for i in range(flags.shape[0]):
        flags[i] = jnp.broadcast_to(pattern_ref[me, i].astype(jnp.float32), flags.shape[1:])
    for d, row in enumerate((row_x, row_y, row_far)):
        for k in range(cols):
            place = column.at[row * cols + k]
            remote(place, place, column_send.at[d, k], column_recv.at[d, k], row, k).wait_recv()
    for step in range(1, cols):
        k = (c + step) % cols
        remote(to_own.at[k], from_own.at[k], own_send.at[k], own_recv.at[k], r, k).wait_recv()
    loads[2].wait()
    grown = pivot_ref[...]
    for h, source, send, recv, row in ((0, from_x, x_send, x_recv, row_x), (1, from_y, y_send, y_recv, row_y)):
        for k in range(cols):
            remote(source.at[k], source.at[k], send.at[h, k], recv.at[h, k], row, k).wait_recv()
        for j in range(mid):
            panel = []
            value = []
            for s in range(cols):
                value.append(
                    from_own[s, h * mid + j].astype(jnp.float32) + source[s, j].astype(jnp.float32)
                )
                panel.append(column[(h * mid + j) * cols + s])
                base[h * mid + j, s] = value[-1]
            value = jnp.concatenate(value, axis=0)
            high = value.astype(jnp.bfloat16)
            low = (value - high.astype(jnp.float32)).astype(jnp.bfloat16)
            both = lax.dot_general(
                jnp.concatenate(panel, axis=0), jnp.concatenate([high, low], axis=1),
                (((0,), (0,)), ((), ())), preferred_element_type=jnp.float32,
            )
            grown = grown + (both[:, :width] + both[:, width:])
    diag_ref[...] = grown

    for h, send, recv, row in ((0, y_send, y_recv, row_y), (1, x_send, x_recv, row_x)):
        for k in range(cols):
            place = last.at[pl.ds(h * mid, mid), k]
            remote(place, place, send.at[h, k], recv.at[h, k], row, k).wait_recv()
    for copy in started:
        copy.wait_send()


def finish(base, last, column, grown, flags, out_ref, diag_ref):
    rows, cols, share, width = base.shape
    chunk = cols * share // width
    total = grown[...]
    for j in range(rows):
        late = last[j].reshape(cols * share, width)
        value = base[j].reshape(cols * share, width) + late.astype(jnp.float32)
        for q in range(chunk):
            begin = (j * chunk + q) * width
            part = value[q * width:(q + 1) * width] * flags[j * chunk + q, 0:1]
            out_ref[begin:begin + width] = (-part).astype(jnp.bfloat16)
        panel = column[j * cols:(j + 1) * cols].reshape(cols * share, width)
        total = total + lax.dot_general(
            panel, late, (((0,), (0,)), ((), ())), preferred_element_type=jnp.float32
        )
    diag_ref[...] = total


def local(green_blocks, lower_panel, pattern, pivot_inverse):
    rows, cols = lax.axis_size("row"), lax.axis_size("col")
    share, supernodes, width = lower_panel.shape
    blocks = pattern.shape[0]
    mid = rows // 2
    vmem = pl.BlockSpec(memory_space=pltpu.VMEM)
    hbm = pl.BlockSpec(memory_space=pltpu.HBM)
    bf16 = lambda *shape: pltpu.VMEM(shape, jnp.bfloat16)
    dma = lambda *shape: pltpu.SemaphoreType.DMA(shape)
    green = green_blocks.reshape(rows, share, -1)
    buffers = [
        bf16(*green.shape),
        bf16(*lower_panel.shape),
        pltpu.VMEM((share * supernodes, width), jnp.float32),
        pltpu.VMEM((width, width), jnp.float32),
        bf16(cols, supernodes, share, width),
        bf16(2, cols, mid, share, width),
        bf16(2, cols, mid, share, width),
        bf16(cols, rows, share, width),
        bf16(cols, rows, share, width),
        bf16(cols, rows, share, width),
        bf16(cols, rows, share, width),
        bf16(cols, mid, share, width),
        bf16(cols, mid, share, width),
    ]
    held = sum(math.prod(b.shape) * jnp.dtype(b.dtype).itemsize for b in buffers)
    middle = pl.pallas_call(
        functools.partial(exchange, rows, cols),
        out_shape=(
            pltpu.VMEM((rows, cols, share, width), jnp.float32),
            pltpu.VMEM((rows, cols, share, width), jnp.bfloat16),
            pltpu.VMEM((rows * cols, share, width), jnp.bfloat16),
            pltpu.VMEM((width, width), jnp.float32),
            pltpu.VMEM((blocks, 8, width), jnp.float32),
        ),
        in_specs=[hbm] * 4,
        out_specs=(vmem,) * 5,
        scratch_shapes=[pltpu.SMEM(pattern.shape[::-1], pattern.dtype)] + buffers + [
            dma(4), dma(cols), dma(cols), dma(3, cols), dma(3, cols), dma(2), dma(2),
            dma(2, cols), dma(2, cols), dma(2, cols), dma(2, cols), dma(cols), dma(cols),
        ],
        compiler_params=pltpu.CompilerParams(
            collective_id=0, has_side_effects=True, vmem_limit_bytes=held + held // 4 + 4 * 1024 * 1024,
        ),
    )(*(pltpu.with_memory_space_constraint(a, pltpu.HBM) for a in (pattern.T, green, lower_panel, pivot_inverse.reshape(width, width))))
    out, diag = pl.pallas_call(
        finish,
        out_shape=(
            jax.ShapeDtypeStruct((rows * cols * share, width), jnp.bfloat16),
            jax.ShapeDtypeStruct((width, width), jnp.float32),
        ),
        in_specs=[vmem] * 5,
        out_specs=(vmem, vmem),
        compiler_params=pltpu.CompilerParams(vmem_limit_bytes=16 * 1024 * 1024),
    )(*middle)
    return out.reshape(-1, 1, width), diag.reshape(1, width, width)


def solution(mesh):
    placed = (
        P("pole", "col", None, "row"),
        P(("row", "col"), "pole", None),
        P(),
        P(("row", "col"), "pole", None),
    )
    return jax.shard_map(
        local,
        mesh=mesh,
        in_specs=placed,
        out_specs=(P("pole", ("row", "col"), None), P(("row", "col"), "pole", None)),
        check_vma=False,
    )
```
